32 devices in a mesh: wa: 16 (over z, y, core), gy: 2 (over x).
Axes of the slice: x: 2, y: 2, z: 4, core: 2. Of those that a mesh axis runs over, the one named last changes fastest.
Arguments:
- input_moments: float32 [120, 128, 32], P(None, 'wa', 'gy'), may hold values from -6 to 6
- solid_cell_mask: int32 [128, 32], P('wa', 'gy'), may hold values 0 or 1
- collision_coefficients: float32 [120, 120], replicated, may hold values from -0.5 to 0.5
- relaxation_rates: float32 [120], replicated, may hold values from 0.1 to 1
Outputs:
- final_state: float32 [120, 128, 32], P(None, 'wa', 'gy')
The draws below stay inside these ranges and needn't reach their ends.
All inputs are finite; a program needn't handle non-finite values. No bound on the sum of `solid_cell_mask` on one device may be relied on, other than what follows from the above.
Results may differ from the reference program's by a relative error of at most 0.0003.
Values sent between devices are 32-bit elements; how exact they have to be, the bound alone decides.
No kernel may reach another device: no remote copies, remote signals or barrier semaphores. Data moves between devices by JAX's collectives and lax.ppermute only.
A program may use at most 64 MiB of HBM per device.

```python
import math
import jax
import jax.numpy as jnp
import numpy as np
from jax import lax

DEG = 7
MOMENT_COUNT = 120
ITERS = 2
NX = 128
NY = 32


def touch_ends(drawn, rng, low, top_value):
    spot = [jax.random.randint(jax.random.fold_in(rng, axis), (), 0, length) for axis, length in enumerate(drawn.shape)]
    main_axis = drawn.shape.index(max(drawn.shape))
    next_to = spot[:main_axis] + [(spot[main_axis] + 1) % drawn.shape[main_axis]] + spot[main_axis + 1:]
    return drawn.at[tuple(spot)].set(low).at[tuple(next_to)].set(top_value)


def block_scale(rng, extent, cuts, smallest, largest):
    def one(axis_at, parts):
        draws = jax.random.uniform(jax.random.fold_in(jax.random.fold_in(rng, 6), axis_at), (parts,), jnp.float32, smallest / len(cuts), largest / len(cuts))
        return jnp.repeat(jnp.exp(draws), extent[axis_at] // parts).reshape((-1,) + (1,) * (len(extent) - axis_at - 1))

    gain = one(*cuts[0])
    for cut in cuts[1:]:
        gain = gain * one(*cut)
    return gain


def scatter_about(key, dims, scale, reach, shards=(), kind=jnp.bfloat16):
    values = scale * jax.random.normal(key, dims, jnp.float32)
    if shards:
        values = values * block_scale(key, dims, shards, -0.22, 0.18)
    return jnp.clip(values, -reach, reach).astype(kind)


def setup_inputs(seed: int = 0) -> dict:
    key_list = jax.random.split(jax.random.key(seed), 5)
    return {
        "input_moments": scatter_about(key_list[0], (MOMENT_COUNT, NX, NY), 1.0, 6.0, ((1, 16), (2, 2)), jnp.float32),
        "solid_cell_mask": touch_ends((jax.random.randint(key_list[1], (NX, NY), 0, 8) < 1).astype(jnp.int32), jax.random.fold_in(key_list[1], 1), 0, 1),
        "collision_coefficients": scatter_about(key_list[2], (MOMENT_COUNT, MOMENT_COUNT), MOMENT_COUNT ** -0.5, 0.5, (), jnp.float32),
        "relaxation_rates": jnp.clip(jnp.exp(jax.random.uniform(key_list[3], (MOMENT_COUNT,), jnp.float32, math.log(0.1), math.log(1.0))), 0.1, 1.0),
    }


highest_degree = lax.Precision.HIGHEST
axial_step = 0.2
cross_step = 0.2
collide_step = 0.5

def moment_table():
    entries = []
    for degree_now in range(DEG + 1):
        for first_k in range(degree_now, -1, -1):
            for second_k in range(degree_now - first_k, -1, -1):
                entries.append((first_k, second_k, degree_now - first_k - second_k))
    return entries

def hermite_value(order, point):
    previous = 1.0
    current_moments = point
    for level in range(1, order):
        previous, current_moments = (current_moments, point * current_moments - level * previous)
    return current_moments

def largest_root(order):
    upper = 2.0 * math.sqrt(order) + 1.0
    value_high = hermite_value(order, upper)
    lower = upper
    for trial in range(100000):
        lower = lower - 0.001
        value_low = hermite_value(order, lower)
        if (value_low > 0.0) != (value_high > 0.0):
            break
        upper = lower
        value_high = value_low
    for repeat in range(80):
        middle = 0.5 * (lower + upper)
        value_mid = hermite_value(order, middle)
        if (value_mid > 0.0) == (value_high > 0.0):
            upper = middle
            value_high = value_mid
        else:
            lower = middle
    return 0.5 * (lower + upper)

def coupling(entries, lookup, direction):
    matrix = np.zeros((len(entries), len(entries)), dtype=np.float32)
    for position, moment in enumerate(entries):
        raised = list(moment)
        raised[direction] += 1
        raised = tuple(raised)
        if raised in lookup:
            partner = lookup[raised]
            matrix[position, partner] = math.sqrt(moment[direction] + 1)
            matrix[partner, position] = math.sqrt(moment[direction] + 1)
    return matrix

def to_float(table):
    return jnp.asarray(table, dtype=jnp.float32)

def operator_tables():
    entries = moment_table()
    number = len(entries)
    lookup = {moment: position for position, moment in enumerate(entries)}
    axial_matrix = coupling(entries, lookup, 0)
    cross_matrix = coupling(entries, lookup, 1)
    degrees = np.array([sum(moment) for moment in entries])
    degree_band_mask = ((np.abs(degrees[:, None] - degrees[None, :]) <= 1) & (degrees[:, None] >= 2) & (degrees[None, :] >= 2)).astype(np.float32)
    unit_rows = [lookup[1, 0, 0], lookup[0, 1, 0], lookup[0, 0, 1]]
    first_selection = np.zeros((number, number), dtype=np.float32)
    second_selection = np.zeros((number, number), dtype=np.float32)
    moment_weights = np.zeros(number, dtype=np.float32)
    for position, moment in enumerate(entries):
        if sum(moment) == 2:
            raised = [direction for direction in range(3) for repeat in range(moment[direction])]
            first_selection[position, unit_rows[raised[0]]] = 1.0
            second_selection[position, unit_rows[raised[1]]] = 1.0
            moment_weights[position] = 1.0 / math.sqrt(2.0) if raised[0] == raised[1] else 1.0
    relaxed = (degrees >= 2).astype(np.float32)
    density = (degrees == 0).astype(np.float32)
    speed_bound = largest_root(DEG + 1)
    return (to_float(axial_matrix), to_float(cross_matrix), to_float(degree_band_mask), to_float(first_selection), to_float(second_selection), to_float(moment_weights), to_float(relaxed), to_float(density), speed_bound)

def wave_numbers(length):
    position = jnp.arange(length, dtype=jnp.int32)
    signed = jnp.where(position < length // 2, position, position - length)
    return signed.astype(jnp.float32) * (axial_step * 2.0 * math.pi / length)

def phase_series(real_part, imag_part, axial_matrix, wave_scale):
    total_real, total_imag = (real_part, imag_part)
    term_real, term_imag = (real_part, imag_part)
    for term_order in range(1, 5):
        pushed_real = jnp.einsum('js,suv->juv', axial_matrix, term_real, precision=highest_degree) * wave_scale[None, :, None]
        pushed_imag = jnp.einsum('js,suv->juv', axial_matrix, term_imag, precision=highest_degree) * wave_scale[None, :, None]
        term_real, term_imag = (pushed_imag / term_order, -pushed_real / term_order)
        total_real = total_real + term_real
        total_imag = total_imag + term_imag
    return (total_real, total_imag)

def cross_update(current_moments, lower_rim, upper_rim, cross_matrix, speed_bound):
    central = jnp.einsum('js,suv->juv', cross_matrix, upper_rim - lower_rim, precision=highest_degree)
    return current_moments - cross_step * (0.5 * central - 0.5 * speed_bound * (upper_rim - 2.0 * current_moments + lower_rim))

def apply_walls(current_moments, mask_float, density):
    return current_moments * (1.0 - mask_float[None, :, :] * (1.0 - density)[:, None, None])

def apply_collisions(current_moments, collision_band, first_selection, second_selection, moment_weights, relaxation_applied):
    first_part = jnp.einsum('js,suv->juv', first_selection, current_moments, precision=highest_degree)
    second_part = jnp.einsum('js,suv->juv', second_selection, current_moments, precision=highest_degree)
    target = moment_weights[:, None, None] * first_part * second_part
    moment_mixing = jnp.einsum('js,suv->juv', collision_band, current_moments, precision=highest_degree)
    return current_moments + collide_step * (moment_mixing - relaxation_applied[:, None, None] * (current_moments - target))

def reference(input_moments, solid_cell_mask, collision_coefficients, relaxation_rates):
    axial_matrix, cross_matrix, degree_band_mask, first_selection, second_selection, moment_weights, relaxed, density, speed_bound = operator_tables()
    collision_band = collision_coefficients * degree_band_mask
    relaxation_applied = relaxation_rates * relaxed
    length = input_moments.shape[1]
    wave_scale = wave_numbers(length)
    mask_float = solid_cell_mask.astype(jnp.float32)
    current_moments = input_moments
    for step_index in range(ITERS):
        spectrum = jnp.fft.fft(current_moments, axis=1)
        real_part = jnp.real(spectrum).astype(jnp.float32)
        imag_part = jnp.imag(spectrum).astype(jnp.float32)
        total_real, total_imag = phase_series(real_part, imag_part, axial_matrix, wave_scale)
        current_moments = jnp.real(jnp.fft.ifft(lax.complex(total_real, total_imag), axis=1)).astype(jnp.float32)
        padded = jnp.pad(current_moments, ((0, 0), (0, 0), (1, 1)))
        current_moments = cross_update(current_moments, padded[:, :, :-2], padded[:, :, 2:], cross_matrix, speed_bound)
        current_moments = apply_walls(current_moments, mask_float, density)
        current_moments = apply_collisions(current_moments, collision_band, first_selection, second_selection, moment_weights, relaxation_applied)
    return current_moments
```

```python
import functools
import math

import jax
import jax.numpy as jnp
import numpy as np
from jax import lax
from jax.experimental import pallas as pl
from jax.experimental.pallas import tpu as pltpu
from jax.sharding import PartitionSpec as P

DEG = 7
ITERS = 2


highest_degree = lax.Precision.HIGHEST
axial_step = 0.2
cross_step = 0.2
collide_step = 0.5


def shifted(value, axis, by):
    count = lax.axis_size(axis)
    return lax.ppermute(value, axis, [(i, (i + by) % count) for i in range(count)])


def from_behind(value, axis, by):
    count = lax.axis_size(axis)
    pairs = [(i, i + by) for i in range(count) if 0 <= i + by < count]
    return lax.ppermute(value, axis, pairs)


def moment_table():
    entries = []
    for degree_now in range(DEG + 1):
        for first_k in range(degree_now, -1, -1):
            for second_k in range(degree_now - first_k, -1, -1):
                entries.append((first_k, second_k, degree_now - first_k - second_k))
    return entries


def hermite_value(order, point):
    previous = 1.0
    current_moments = point
    for level in range(1, order):
        previous, current_moments = (current_moments, point * current_moments - level * previous)
    return current_moments


def largest_root(order):
    upper = 2.0 * math.sqrt(order) + 1.0
    value_high = hermite_value(order, upper)
    lower = upper
    for trial in range(100000):
        lower = lower - 0.001
        value_low = hermite_value(order, lower)
        if (value_low > 0.0) != (value_high > 0.0):
            break
        upper = lower
        value_high = value_low
    for repeat in range(80):
        middle = 0.5 * (lower + upper)
        value_mid = hermite_value(order, middle)
        if (value_mid > 0.0) == (value_high > 0.0):
            upper = middle
            value_high = value_mid
        else:
            lower = middle
    return 0.5 * (lower + upper)


def coupling(entries, lookup, direction):
    matrix = np.zeros((len(entries), len(entries)), dtype=np.float32)
    for position, moment in enumerate(entries):
        raised = list(moment)
        raised[direction] += 1
        raised = tuple(raised)
        if raised in lookup:
            partner = lookup[raised]
            matrix[position, partner] = math.sqrt(moment[direction] + 1)
            matrix[partner, position] = math.sqrt(moment[direction] + 1)
    return matrix


def to_float(table):
    return jnp.asarray(table, dtype=jnp.float32)


def operator_tables():
    entries = moment_table()
    number = len(entries)
    lookup = {moment: position for position, moment in enumerate(entries)}
    axial_matrix = coupling(entries, lookup, 0)
    cross_matrix = coupling(entries, lookup, 1)
    degrees = np.array([sum(moment) for moment in entries])
    degree_band_mask = (
        (np.abs(degrees[:, None] - degrees[None, :]) <= 1)
        & (degrees[:, None] >= 2)
        & (degrees[None, :] >= 2)
    ).astype(np.float32)
    unit_rows = [lookup[1, 0, 0], lookup[0, 1, 0], lookup[0, 0, 1]]
    first_selection = np.zeros((number, number), dtype=np.float32)
    second_selection = np.zeros((number, number), dtype=np.float32)
    moment_weights = np.zeros(number, dtype=np.float32)
    for position, moment in enumerate(entries):
        if sum(moment) == 2:
            raised = [direction for direction in range(3) for repeat in range(moment[direction])]
            first_selection[position, unit_rows[raised[0]]] = 1.0
            second_selection[position, unit_rows[raised[1]]] = 1.0
            moment_weights[position] = 1.0 / math.sqrt(2.0) if raised[0] == raised[1] else 1.0
    relaxed = (degrees >= 2).astype(np.float32)
    density = (degrees == 0).astype(np.float32)
    speed_bound = largest_root(DEG + 1)
    return (
        to_float(axial_matrix),
        to_float(cross_matrix),
        to_float(degree_band_mask),
        to_float(first_selection),
        to_float(second_selection),
        to_float(moment_weights),
        to_float(relaxed),
        to_float(density),
        speed_bound,
    )


def wave_numbers(length):
    position = jnp.arange(length, dtype=jnp.int32)
    signed = jnp.where(position < length // 2, position, position - length)
    return signed.astype(jnp.float32) * (axial_step * 2.0 * math.pi / length)


def fourier_tables(length):
    position = jnp.arange(length, dtype=jnp.int32)
    phase_index = position[:, None] * position[None, :] % length
    angles = phase_index.astype(jnp.float32) * (2.0 * math.pi / length)
    return (jnp.cos(angles), jnp.sin(angles))


def phase_series(real_part, imag_part, axial_matrix, wave_scale):
    total_real, total_imag = (real_part, imag_part)
    term_real, term_imag = (real_part, imag_part)
    for term_order in range(1, 5):
        pushed_real = (
            jnp.einsum("js,suv->juv", axial_matrix, term_real, precision=highest_degree)
            * wave_scale[None, :, None]
        )
        pushed_imag = (
            jnp.einsum("js,suv->juv", axial_matrix, term_imag, precision=highest_degree)
            * wave_scale[None, :, None]
        )
        term_real, term_imag = (pushed_imag / term_order, -pushed_real / term_order)
        total_real = total_real + term_real
        total_imag = total_imag + term_imag
    return (total_real, total_imag)


def axial_update(line_field, cosine_table, sine_table, axial_matrix, wave_scale):
    length = line_field.shape[1]
    real_part = jnp.einsum("mxl,xk->mkl", line_field, cosine_table, precision=highest_degree)
    imag_part = -jnp.einsum("mxl,xk->mkl", line_field, sine_table, precision=highest_degree)
    total_real, total_imag = phase_series(real_part, imag_part, axial_matrix, wave_scale)
    restored = jnp.einsum("mkl,kx->mxl", total_real, cosine_table, precision=highest_degree)
    restored = restored - jnp.einsum(
        "mkl,kx->mxl", total_imag, sine_table, precision=highest_degree
    )
    return restored / length


def cross_update(current_moments, lower_rim, upper_rim, cross_matrix, speed_bound):
    central = jnp.einsum(
        "js,suv->juv", cross_matrix, upper_rim - lower_rim, precision=highest_degree
    )
    return current_moments - cross_step * (
        0.5 * central - 0.5 * speed_bound * (upper_rim - 2.0 * current_moments + lower_rim)
    )


def apply_walls(current_moments, mask_float, density):
    return current_moments * (1.0 - mask_float[None, :, :] * (1.0 - density)[:, None, None])


def apply_collisions(
    current_moments,
    collision_band,
    first_selection,
    second_selection,
    moment_weights,
    relaxation_applied,
):
    first_part = jnp.einsum(
        "js,suv->juv", first_selection, current_moments, precision=highest_degree
    )
    second_part = jnp.einsum(
        "js,suv->juv", second_selection, current_moments, precision=highest_degree
    )
    target = moment_weights[:, None, None] * first_part * second_part
    moment_mixing = jnp.einsum(
        "js,suv->juv", collision_band, current_moments, precision=highest_degree
    )
    return current_moments + collide_step * (
        moment_mixing - relaxation_applied[:, None, None] * (current_moments - target)
    )


def local(input_moments, solid_cell_mask, collision_coefficients, relaxation_rates):
    (
        axial_matrix,
        cross_matrix,
        degree_band_mask,
        first_selection,
        second_selection,
        moment_weights,
        relaxed,
        density,
        speed_bound,
    ) = operator_tables()
    collision_band = collision_coefficients * degree_band_mask
    relaxation_applied = relaxation_rates * relaxed
    length = input_moments.shape[1] * lax.axis_size("wa")
    cosine_table, sine_table = fourier_tables(length)
    wave_scale = wave_numbers(length)
    line_field = lax.all_to_all(input_moments, "wa", split_axis=2, concat_axis=1, tiled=True)
    mask_float = lax.all_to_all(
        solid_cell_mask, "wa", split_axis=1, concat_axis=0, tiled=True
    ).astype(jnp.float32)
    position_wa = lax.axis_index("wa")
    last_wa = lax.axis_size("wa") - 1
    for step_index in range(ITERS):
        line_field = axial_update(line_field, cosine_table, sine_table, axial_matrix, wave_scale)
        from_lower = shifted(line_field[:, :, -1:], "wa", 1)
        across_lower = from_behind(from_lower, "gy", 1)
        lower_line = jnp.where(position_wa == 0, across_lower, from_lower)
        from_upper = shifted(line_field[:, :, :1], "wa", -1)
        across_upper = from_behind(from_upper, "gy", -1)
        upper_line = jnp.where(position_wa == last_wa, across_upper, from_upper)
        padded = jnp.concatenate([lower_line, line_field, upper_line], axis=2)
        line_field = cross_update(
            line_field, padded[:, :, :-2], padded[:, :, 2:], cross_matrix, speed_bound
        )
        line_field = apply_walls(line_field, mask_float, density)
        line_field = apply_collisions(
            line_field,
            collision_band,
            first_selection,
            second_selection,
            moment_weights,
            relaxation_applied,
        )
    return lax.all_to_all(line_field, "wa", split_axis=1, concat_axis=2, tiled=True)


LANES = 128
HALO = ITERS
TERMS = 4
bfloat = jnp.bfloat16


def lane_tables():
    entries = moment_table()
    number = len(entries)
    lookup = {moment: position for position, moment in enumerate(entries)}
    order = sorted(entries, key=lambda k: (k[1] + k[2], k[2], k[0]))
    lane_of = {moment: lane for lane, moment in enumerate(order)}
    place = np.zeros((LANES, LANES), np.float32)
    for moment in entries:
        place[lookup[moment], lane_of[moment]] = 1.0
    place[number, number] = 1.0
    rows = np.zeros((8, LANES), np.float32)
    for moment in entries:
        lane = lane_of[moment]
        rows[0, lane] = math.sqrt(moment[0])
        if sum(moment) < DEG:
            rows[1, lane] = math.sqrt(moment[0] + 1)
        rows[2, lane] = 1.0 if sum(moment) > 0 else 0.0
        rows[3, lane] = 1.0 if sum(moment) >= 2 else 0.0
    cross = place[:number].T @ coupling(entries, lookup, 1) @ place[:number]
    first = np.zeros((LANES, LANES), np.float32)
    second = np.zeros((LANES, LANES), np.float32)
    units = [lane_of[1, 0, 0], lane_of[0, 1, 0], lane_of[0, 0, 1]]
    for moment in entries:
        if sum(moment) == 2:
            raised = [d for d in range(3) for repeat in range(moment[d])]
            first[units[raised[0]], lane_of[moment]] = 1.0
            second[units[raised[1]], lane_of[moment]] = 1.0
            rows[4, lane_of[moment]] = 1.0 / math.sqrt(2.0) if raised[0] == raised[1] else 1.0
    degrees = np.array([sum(moment) for moment in entries])
    band = (
        (np.abs(degrees[:, None] - degrees[None, :]) <= 1)
        & (degrees[:, None] >= 2)
        & (degrees[None, :] >= 2)
    ).astype(np.float32)
    return place, rows, cross, first, second, band


def halves(table):
    high = np.asarray(table, np.float32).astype(bfloat)
    low = (np.asarray(table, np.float32) - high.astype(np.float32)).astype(bfloat)
    return high, low


def split(value):
    high = value.astype(bfloat)
    low = (value - high.astype(jnp.float32)).astype(bfloat)
    return high, low


def derivative_tables(length):
    wave = np.arange(length)
    signed = np.where(wave < length // 2, wave, wave - length)
    scale = signed * (axial_step * 2.0 * math.pi / length)
    distance = np.arange(length)
    phase = np.exp(2j * np.pi * (wave[:, None] * distance[None, :] % length) / length)
    offset = (distance[:, None] - distance[None, :]) % length
    blocks = []
    for term in range(1, TERMS + 1):
        series = ((-1j * scale) ** term)[:, None] * phase / math.factorial(term)
        profile = series.sum(axis=0).real / length
        blocks.append(profile[offset])
    return np.concatenate(blocks, axis=0).astype(np.float32)


def pack_kernel(where_ref, field_ref, mask_ref, place_ref, block_ref, rim_ref):
    count, cells, lines = field_ref.shape
    row = lax.broadcasted_iota(jnp.int32, (LANES - count, lines), 0)
    for cell in range(cells):
        flags = mask_ref[cell : cell + 1, :].astype(jnp.float32)
        tail = jnp.where(row == 0, jnp.broadcast_to(flags, row.shape), 0.0)
        stacked = jnp.concatenate([field_ref[:, cell, :], tail], axis=0)
        block_ref[:, cell, :] = lax.dot_general(
            stacked,
            place_ref[...],
            (((0,), (0,)), ((), ())),
            precision=highest_degree,
            preferred_element_type=jnp.float32,
        )
    start = jnp.where(where_ref[1] == 0, lines - HALO, 0)
    rim_ref[...] = block_ref[pl.ds(start, HALO)]


def prepare_kernel(mixing_ref, band_ref, rates_ref, rows_ref, place_ref, select_ref, table_ref, rate_ref):
    count = mixing_ref.shape[0]
    place = place_ref[0:count, :]
    banded = mixing_ref[...] * band_ref[...]
    half = lax.dot_general(
        banded, place, (((0,), (0,)), ((), ())), precision=highest_degree,
        preferred_element_type=jnp.float32,
    )
    mixed = lax.dot_general(
        place, half, (((0,), (0,)), ((), ())), precision=highest_degree,
        preferred_element_type=jnp.float32,
    )
    high, low = split(mixed)
    table_ref[0:LANES, 0:LANES] = high
    table_ref[LANES:, 0:LANES] = high
    table_ref[0:LANES, LANES : 2 * LANES] = low
    table_ref[LANES:, LANES : 2 * LANES] = jnp.zeros_like(low)
    table_ref[:, 2 * LANES :] = select_ref[...]
    rates = jnp.broadcast_to(rates_ref[...], (8, count))
    lanes = lax.dot_general(
        rates, place, (((1,), (0,)), ((), ())), precision=highest_degree,
        preferred_element_type=jnp.float32,
    )
    rate_ref[...] = lanes * rows_ref[3:4, :]


def mix_axial(value, rows_ref):
    down = pltpu.roll(value, 1, 1)
    up = pltpu.roll(value, LANES - 1, 1)
    return rows_ref[0:1, :] * down + rows_ref[1:2, :] * up


def cross_and_collide(lower, middle, upper, flags, rows_ref, rate_ref, cross_ref, table_ref, bound):
    high, low = split(upper - lower)
    pair = jnp.dot(
        jnp.concatenate([high, low], axis=1), cross_ref[...], preferred_element_type=jnp.float32
    )
    central = pair[:, :LANES] + pair[:, LANES:]
    moved = middle - cross_step * (
        0.5 * central - 0.5 * bound * (upper - 2.0 * middle + lower)
    )
    moved = moved * (1.0 - flags * rows_ref[2:3, :])
    high, low = split(moved)
    sums = jnp.dot(
        jnp.concatenate([high, low], axis=1), table_ref[...], preferred_element_type=jnp.float32
    )
    mixing = sums[:, :LANES] + sums[:, LANES : 2 * LANES]
    target = rows_ref[4:5, :] * sums[:, 2 * LANES : 3 * LANES] * sums[:, 3 * LANES :]
    return moved + collide_step * (mixing - rate_ref[0:1, :] * (moved - target))


def march_kernel(
    where_ref, held_ref, last_ref, deriv_ref, small_ref, rows_ref, rate_ref, cross_ref, table_ref,
    place_ref, out_ref, field, moved, after, ends, final, *, reach, chunk, bound
):
    me, slab = where_ref[0], where_ref[1]
    flag_lane, cells, lines = out_ref.shape
    length = field.shape[1]
    rim_slot = jnp.where(slab == 0, lines + HALO, 0)
    half = held_ref.shape[0]
    for entry, offset in enumerate(reach):
        source = held_ref.at[entry] if entry < half else last_ref.at[entry - half]
        start = pl.multiple_of((me ^ offset) * cells, cells)
        field[HALO : HALO + lines, pl.ds(start, cells), :] = source[0:lines]
        field[pl.ds(rim_slot, HALO), pl.ds(start, cells), :] = source[lines:]

    zero = jnp.zeros((length, LANES), jnp.float32)
    moved[HALO - 1] = zero
    moved[HALO + lines] = zero
    first_slot = jnp.where(slab == 0, HALO, 0)
    width = 2
    total = lines + HALO
    for position in range(0, total, width):
        columns = [first_slot + position + k for k in range(min(width, total - position))]
        values = [field[column] for column in columns]
        high, low = split(jnp.concatenate(values, axis=1))
        series = jnp.dot(
            deriv_ref[...],
            jnp.concatenate([high, low, high], axis=0),
            preferred_element_type=jnp.float32,
        )
        for k, column in enumerate(columns):
            part = series[:, k * LANES : (k + 1) * LANES]
            term = part[(TERMS - 1) * length :]
            for n in range(TERMS - 2, -1, -1):
                term = part[n * length : (n + 1) * length] + mix_axial(term, rows_ref)
            moved[column] = values[k] + mix_axial(term, rows_ref)

    start_slot = HALO - slab
    total = lines + 1
    for position in range(0, total, chunk):
        size = min(chunk, total - position)
        base = start_slot + position
        flat = (size * length, LANES)
        lower = moved[pl.ds(base - 1, size)].reshape(flat)
        middle = moved[pl.ds(base, size)].reshape(flat)
        upper = moved[pl.ds(base + 1, size)].reshape(flat)
        flags = field[pl.ds(base, size)].reshape(flat)[:, flag_lane : flag_lane + 1]
        result = cross_and_collide(
            lower, middle, upper, flags, rows_ref, rate_ref, cross_ref, table_ref, bound
        )
        after[pl.ds(base, size)] = result.reshape(size, length, LANES)

    own = pl.multiple_of(me * cells, cells)
    taps = jnp.concatenate(
        [small_ref[pl.ds(n * length + own, cells), :] for n in range(TERMS)], axis=0
    )
    high, low = split(taps)
    taps = jnp.concatenate([high, high, low], axis=1)
    blank = jnp.zeros((cells, LANES), jnp.float32)
    ends[HALO - 1] = blank
    ends[HALO + lines] = blank
    for position in range(0, total, width):
        columns = [start_slot + position + k for k in range(min(width, total - position))]
        values = [after[column] for column in columns]
        high, low = split(jnp.concatenate(values, axis=1) if len(values) > 1 else values[0])
        series = jnp.dot(
            taps, jnp.concatenate([high, low, high], axis=0), preferred_element_type=jnp.float32
        )
        for k, column in enumerate(columns):
            part = series[:, k * LANES : (k + 1) * LANES]
            term = part[(TERMS - 1) * cells :]
            for n in range(TERMS - 2, -1, -1):
                term = part[n * cells : (n + 1) * cells] + mix_axial(term, rows_ref)
            ends[column] = after[column, pl.ds(own, cells), :] + mix_axial(term, rows_ref)

    flat = (lines * cells, LANES)
    flags = held_ref[0, 0:lines].reshape(flat)[:, flag_lane : flag_lane + 1]
    result = cross_and_collide(
        ends[HALO - 1 : HALO - 1 + lines].reshape(flat),
        ends[HALO : HALO + lines].reshape(flat),
        ends[HALO + 1 : HALO + 1 + lines].reshape(flat),
        flags, rows_ref, rate_ref, cross_ref, table_ref, bound,
    )
    final[...] = result.reshape(lines, cells, LANES)
    place = place_ref[0:flag_lane, :]
    for cell in range(cells):
        out_ref[:, cell, :] = lax.dot_general(
            place, final[:, cell, :], (((1,), (1,)), ((), ())), precision=highest_degree,
            preferred_element_type=jnp.float32,
        )


def gathered(input_moments, solid_cell_mask, collision_coefficients, relaxation_rates):
    count, cells, lines = input_moments.shape
    ranks = lax.axis_size("wa")
    length = cells * ranks
    place, rows, cross, first, second, band = lane_tables()
    bound = largest_root(DEG + 1)
    deriv = derivative_tables(length)
    deriv_high, deriv_low = halves(deriv)
    wide = np.concatenate([deriv_high, deriv_high, deriv_low], axis=1)
    cross_high, cross_low = halves(cross.T)
    cross_wide = np.block([[cross_high, cross_low], [cross_high, np.zeros_like(cross_low)]])
    picks = np.concatenate([first, second], axis=1).astype(bfloat)
    picks = np.concatenate([picks, picks], axis=0)
    where = jnp.stack([lax.axis_index("wa"), lax.axis_index("gy")]).astype(jnp.int32)
    smem = pl.BlockSpec(memory_space=pltpu.SMEM)
    vmem = pl.BlockSpec(memory_space=pltpu.VMEM)
    float32 = jnp.float32
    block, rim = pl.pallas_call(
        pack_kernel,
        out_shape=(
            jax.ShapeDtypeStruct((lines, cells, LANES), float32),
            jax.ShapeDtypeStruct((HALO, cells, LANES), float32),
        ),
        in_specs=[smem, vmem, vmem, vmem],
        out_specs=(vmem, vmem),
        name="pack",
    )(where, input_moments, solid_cell_mask, place)
    table, rate = pl.pallas_call(
        prepare_kernel,
        out_shape=(
            jax.ShapeDtypeStruct((2 * LANES, 4 * LANES), bfloat),
            jax.ShapeDtypeStruct((8, LANES), float32),
        ),
        in_specs=[vmem] * 6,
        out_specs=(vmem, vmem),
        name="prepare",
    )(collision_coefficients, band, relaxation_rates.reshape(1, count), rows, place, picks)

    slabs = lax.axis_size("gy")
    rim = lax.ppermute(rim, "gy", [(i, i ^ 1) for i in range(slabs)])
    held = jnp.concatenate([block, rim], axis=0)[None]
    reach = [0]
    bit = ranks // 2
    while bit:
        got = lax.ppermute(held, "wa", [(i, i ^ bit) for i in range(ranks)])
        reach += [offset ^ bit for offset in reach]
        bit //= 2
        if bit:
            held = jnp.concatenate([held, got], axis=0)
    slots = lines + 2 * HALO
    return pl.pallas_call(
        functools.partial(march_kernel, reach=tuple(reach), chunk=6, bound=bound),
        out_shape=jax.ShapeDtypeStruct(input_moments.shape, float32),
        in_specs=[smem] + [vmem] * 9,
        out_specs=vmem,
        scratch_shapes=[
            pltpu.VMEM((slots, length, LANES), float32),
            pltpu.VMEM((slots, length, LANES), float32),
            pltpu.VMEM((slots, length, LANES), float32),
            pltpu.VMEM((slots, cells, LANES), float32),
            pltpu.VMEM((lines, cells, LANES), float32),
        ],
        name="march",
    )(where, held, got, wide, deriv, rows, rate, cross_wide, table, place)


def gathers(sizes, shape):
    ranks, slabs = sizes["wa"], sizes["gy"]
    cells, lines = shape[1] // ranks, shape[2] // slabs
    slab_bytes = 4 * LANES * shape[1] * (lines + 2 * HALO)
    return (
        slabs == 2
        and ranks > 1
        and ranks & (ranks - 1) == 0
        and cells % 8 == 0
        and lines >= HALO
        and shape[0] < LANES
        and 6 * slab_bytes <= 40 * 2**20
    )


def solution(mesh):
    in_specs = (P(None, "wa", "gy"), P("wa", "gy"), P(), P())
    out_specs = P(None, "wa", "gy")

    def program(input_moments, *others):
        body = gathered if gathers(mesh.shape, input_moments.shape) else local
        mapped = jax.shard_map(
            body, mesh=mesh, in_specs=in_specs, out_specs=out_specs, check_vma=False
        )
        return mapped(input_moments, *others)

    return program
```

```python
import functools
import math

import jax
import jax.numpy as jnp
import numpy as np
from jax import lax
from jax.experimental import pallas as pl
from jax.experimental.pallas import tpu as pltpu
from jax.sharding import PartitionSpec as P

DEG = 7
ITERS = 2


highest_degree = lax.Precision.HIGHEST
axial_step = 0.2
cross_step = 0.2
collide_step = 0.5


def shifted(value, axis, by):
    count = lax.axis_size(axis)
    return lax.ppermute(value, axis, [(i, (i + by) % count) for i in range(count)])


def from_behind(value, axis, by):
    count = lax.axis_size(axis)
    pairs = [(i, i + by) for i in range(count) if 0 <= i + by < count]
    return lax.ppermute(value, axis, pairs)


def moment_table():
    entries = []
    for degree_now in range(DEG + 1):
        for first_k in range(degree_now, -1, -1):
            for second_k in range(degree_now - first_k, -1, -1):
                entries.append((first_k, second_k, degree_now - first_k - second_k))
    return entries


def hermite_value(order, point):
    previous = 1.0
    current_moments = point
    for level in range(1, order):
        previous, current_moments = (current_moments, point * current_moments - level * previous)
    return current_moments


def largest_root(order):
    upper = 2.0 * math.sqrt(order) + 1.0
    value_high = hermite_value(order, upper)
    lower = upper
    for trial in range(100000):
        lower = lower - 0.001
        value_low = hermite_value(order, lower)
        if (value_low > 0.0) != (value_high > 0.0):
            break
        upper = lower
        value_high = value_low
    for repeat in range(80):
        middle = 0.5 * (lower + upper)
        value_mid = hermite_value(order, middle)
        if (value_mid > 0.0) == (value_high > 0.0):
            upper = middle
            value_high = value_mid
        else:
            lower = middle
    return 0.5 * (lower + upper)


def coupling(entries, lookup, direction):
    matrix = np.zeros((len(entries), len(entries)), dtype=np.float32)
    for position, moment in enumerate(entries):
        raised = list(moment)
        raised[direction] += 1
        raised = tuple(raised)
        if raised in lookup:
            partner = lookup[raised]
            matrix[position, partner] = math.sqrt(moment[direction] + 1)
            matrix[partner, position] = math.sqrt(moment[direction] + 1)
    return matrix


def to_float(table):
    return jnp.asarray(table, dtype=jnp.float32)


def operator_tables():
    entries = moment_table()
    number = len(entries)
    lookup = {moment: position for position, moment in enumerate(entries)}
    axial_matrix = coupling(entries, lookup, 0)
    cross_matrix = coupling(entries, lookup, 1)
    degrees = np.array([sum(moment) for moment in entries])
    degree_band_mask = (
        (np.abs(degrees[:, None] - degrees[None, :]) <= 1)
        & (degrees[:, None] >= 2)
        & (degrees[None, :] >= 2)
    ).astype(np.float32)
    unit_rows = [lookup[1, 0, 0], lookup[0, 1, 0], lookup[0, 0, 1]]
    first_selection = np.zeros((number, number), dtype=np.float32)
    second_selection = np.zeros((number, number), dtype=np.float32)
    moment_weights = np.zeros(number, dtype=np.float32)
    for position, moment in enumerate(entries):
        if sum(moment) == 2:
            raised = [direction for direction in range(3) for repeat in range(moment[direction])]
            first_selection[position, unit_rows[raised[0]]] = 1.0
            second_selection[position, unit_rows[raised[1]]] = 1.0
            moment_weights[position] = 1.0 / math.sqrt(2.0) if raised[0] == raised[1] else 1.0
    relaxed = (degrees >= 2).astype(np.float32)
    density = (degrees == 0).astype(np.float32)
    speed_bound = largest_root(DEG + 1)
    return (
        to_float(axial_matrix),
        to_float(cross_matrix),
        to_float(degree_band_mask),
        to_float(first_selection),
        to_float(second_selection),
        to_float(moment_weights),
        to_float(relaxed),
        to_float(density),
        speed_bound,
    )


def wave_numbers(length):
    position = jnp.arange(length, dtype=jnp.int32)
    signed = jnp.where(position < length // 2, position, position - length)
    return signed.astype(jnp.float32) * (axial_step * 2.0 * math.pi / length)


def fourier_tables(length):
    position = jnp.arange(length, dtype=jnp.int32)
    phase_index = position[:, None] * position[None, :] % length
    angles = phase_index.astype(jnp.float32) * (2.0 * math.pi / length)
    return (jnp.cos(angles), jnp.sin(angles))


def phase_series(real_part, imag_part, axial_matrix, wave_scale):
    total_real, total_imag = (real_part, imag_part)
    term_real, term_imag = (real_part, imag_part)
    for term_order in range(1, 5):
        pushed_real = (
            jnp.einsum("js,suv->juv", axial_matrix, term_real, precision=highest_degree)
            * wave_scale[None, :, None]
        )
        pushed_imag = (
            jnp.einsum("js,suv->juv", axial_matrix, term_imag, precision=highest_degree)
            * wave_scale[None, :, None]
        )
        term_real, term_imag = (pushed_imag / term_order, -pushed_real / term_order)
        total_real = total_real + term_real
        total_imag = total_imag + term_imag
    return (total_real, total_imag)


def axial_update(line_field, cosine_table, sine_table, axial_matrix, wave_scale):
    length = line_field.shape[1]
    real_part = jnp.einsum("mxl,xk->mkl", line_field, cosine_table, precision=highest_degree)
    imag_part = -jnp.einsum("mxl,xk->mkl", line_field, sine_table, precision=highest_degree)
    total_real, total_imag = phase_series(real_part, imag_part, axial_matrix, wave_scale)
    restored = jnp.einsum("mkl,kx->mxl", total_real, cosine_table, precision=highest_degree)
    restored = restored - jnp.einsum(
        "mkl,kx->mxl", total_imag, sine_table, precision=highest_degree
    )
    return restored / length


def cross_update(current_moments, lower_rim, upper_rim, cross_matrix, speed_bound):
    central = jnp.einsum(
        "js,suv->juv", cross_matrix, upper_rim - lower_rim, precision=highest_degree
    )
    return current_moments - cross_step * (
        0.5 * central - 0.5 * speed_bound * (upper_rim - 2.0 * current_moments + lower_rim)
    )


def apply_walls(current_moments, mask_float, density):
    return current_moments * (1.0 - mask_float[None, :, :] * (1.0 - density)[:, None, None])


def apply_collisions(
    current_moments,
    collision_band,
    first_selection,
    second_selection,
    moment_weights,
    relaxation_applied,
):
    first_part = jnp.einsum(
        "js,suv->juv", first_selection, current_moments, precision=highest_degree
    )
    second_part = jnp.einsum(
        "js,suv->juv", second_selection, current_moments, precision=highest_degree
    )
    target = moment_weights[:, None, None] * first_part * second_part
    moment_mixing = jnp.einsum(
        "js,suv->juv", collision_band, current_moments, precision=highest_degree
    )
    return current_moments + collide_step * (
        moment_mixing - relaxation_applied[:, None, None] * (current_moments - target)
    )


def local(input_moments, solid_cell_mask, collision_coefficients, relaxation_rates):
    (
        axial_matrix,
        cross_matrix,
        degree_band_mask,
        first_selection,
        second_selection,
        moment_weights,
        relaxed,
        density,
        speed_bound,
    ) = operator_tables()
    collision_band = collision_coefficients * degree_band_mask
    relaxation_applied = relaxation_rates * relaxed
    length = input_moments.shape[1] * lax.axis_size("wa")
    cosine_table, sine_table = fourier_tables(length)
    wave_scale = wave_numbers(length)
    line_field = lax.all_to_all(input_moments, "wa", split_axis=2, concat_axis=1, tiled=True)
    mask_float = lax.all_to_all(
        solid_cell_mask, "wa", split_axis=1, concat_axis=0, tiled=True
    ).astype(jnp.float32)
    position_wa = lax.axis_index("wa")
    last_wa = lax.axis_size("wa") - 1
    for step_index in range(ITERS):
        line_field = axial_update(line_field, cosine_table, sine_table, axial_matrix, wave_scale)
        from_lower = shifted(line_field[:, :, -1:], "wa", 1)
        across_lower = from_behind(from_lower, "gy", 1)
        lower_line = jnp.where(position_wa == 0, across_lower, from_lower)
        from_upper = shifted(line_field[:, :, :1], "wa", -1)
        across_upper = from_behind(from_upper, "gy", -1)
        upper_line = jnp.where(position_wa == last_wa, across_upper, from_upper)
        padded = jnp.concatenate([lower_line, line_field, upper_line], axis=2)
        line_field = cross_update(
            line_field, padded[:, :, :-2], padded[:, :, 2:], cross_matrix, speed_bound
        )
        line_field = apply_walls(line_field, mask_float, density)
        line_field = apply_collisions(
            line_field,
            collision_band,
            first_selection,
            second_selection,
            moment_weights,
            relaxation_applied,
        )
    return lax.all_to_all(line_field, "wa", split_axis=1, concat_axis=2, tiled=True)


LANES = 128
HALO = ITERS
TERMS = 4
bfloat = jnp.bfloat16


def lane_tables():
    entries = moment_table()
    number = len(entries)
    lookup = {moment: position for position, moment in enumerate(entries)}
    order = sorted(entries, key=lambda k: (k[1] + k[2], k[2], k[0]))
    lane_of = {moment: lane for lane, moment in enumerate(order)}
    place = np.zeros((LANES, LANES), np.float32)
    for moment in entries:
        place[lookup[moment], lane_of[moment]] = 1.0
    place[number, number] = 1.0
    rows = np.zeros((8, LANES), np.float32)
    for moment in entries:
        lane = lane_of[moment]
        rows[0, lane] = math.sqrt(moment[0])
        if sum(moment) < DEG:
            rows[1, lane] = math.sqrt(moment[0] + 1)
        rows[2, lane] = 1.0 if sum(moment) > 0 else 0.0
        rows[3, lane] = 1.0 if sum(moment) >= 2 else 0.0
    cross = place[:number].T @ coupling(entries, lookup, 1) @ place[:number]
    first = np.zeros((LANES, LANES), np.float32)
    second = np.zeros((LANES, LANES), np.float32)
    units = [lane_of[1, 0, 0], lane_of[0, 1, 0], lane_of[0, 0, 1]]
    for moment in entries:
        if sum(moment) == 2:
            raised = [d for d in range(3) for repeat in range(moment[d])]
            first[units[raised[0]], lane_of[moment]] = 1.0
            second[units[raised[1]], lane_of[moment]] = 1.0
            rows[4, lane_of[moment]] = 1.0 / math.sqrt(2.0) if raised[0] == raised[1] else 1.0
    degrees = np.array([sum(moment) for moment in entries])
    band = (
        (np.abs(degrees[:, None] - degrees[None, :]) <= 1)
        & (degrees[:, None] >= 2)
        & (degrees[None, :] >= 2)
    ).astype(np.float32)
    return place, rows, cross, first, second, band


def halves(table):
    high = np.asarray(table, np.float32).astype(bfloat)
    low = (np.asarray(table, np.float32) - high.astype(np.float32)).astype(bfloat)
    return high, low


def split(value):
    high = value.astype(bfloat)
    low = (value - high.astype(jnp.float32)).astype(bfloat)
    return high, low


def derivative_tables(length):
    wave = np.arange(length)
    signed = np.where(wave < length // 2, wave, wave - length)
    scale = signed * (axial_step * 2.0 * math.pi / length)
    distance = np.arange(length)
    phase = np.exp(2j * np.pi * (wave[:, None] * distance[None, :] % length) / length)
    offset = (distance[:, None] - distance[None, :]) % length
    blocks = []
    for term in range(1, TERMS + 1):
        series = ((-1j * scale) ** term)[:, None] * phase / math.factorial(term)
        profile = series.sum(axis=0).real / length
        blocks.append(profile[offset])
    return np.concatenate(blocks, axis=0).astype(np.float32)


def thirds(value):
    high = value.astype(bfloat)
    rest = value - high.astype(jnp.float32)
    middle = rest.astype(bfloat)
    return high, middle, (rest - middle.astype(jnp.float32)).astype(bfloat)


def permute_lanes(value, place):
    total = None
    for part in thirds(value):
        moved = jnp.dot(part, place, preferred_element_type=jnp.float32)
        total = moved if total is None else total + moved
    return total


def pack_kernel(field_ref, mask_ref, place_ref, block_ref, rim_ref):
    cells, lines, count = field_ref.shape
    rows = field_ref[...].reshape(cells * lines, count)
    packed = permute_lanes(rows, place_ref[0:count, :])
    row = lax.broadcasted_iota(jnp.int32, (lines, lines), 0)
    column = lax.broadcasted_iota(jnp.int32, (lines, lines), 1)
    flags = jnp.concatenate(
        [
            jnp.where(row == column, mask_ref[cell : cell + 1, :].astype(jnp.float32), 0.0)
            for cell in range(cells)
        ],
        axis=0,
    )
    flag_row = jnp.broadcast_to(place_ref[count : count + 1, :], (lines, LANES))
    packed = packed + jnp.dot(flags.astype(bfloat), flag_row, preferred_element_type=jnp.float32)
    for cell in range(cells):
        block_ref[:, cell, :] = packed[cell * lines : (cell + 1) * lines]
    start = jnp.where(lax.axis_index("gy") == 0, lines - HALO, 0)
    rim_ref[...] = block_ref[pl.ds(start, HALO)]


def prepare_kernel(mixing_ref, band_ref, rates_ref, rows_ref, place_ref, select_ref, table_ref, rate_ref):
    count = mixing_ref.shape[0]
    place = place_ref[0:count, :]
    banded = mixing_ref[...] * band_ref[...]
    half = lax.dot_general(
        banded, place, (((0,), (0,)), ((), ())), precision=highest_degree,
        preferred_element_type=jnp.float32,
    )
    mixed = lax.dot_general(
        place, half, (((0,), (0,)), ((), ())), precision=highest_degree,
        preferred_element_type=jnp.float32,
    )
    high, low = split(mixed)
    table_ref[0:LANES, 0:LANES] = high
    table_ref[LANES:, 0:LANES] = high
    table_ref[0:LANES, LANES : 2 * LANES] = low
    table_ref[LANES:, LANES : 2 * LANES] = jnp.zeros_like(low)
    table_ref[:, 2 * LANES :] = select_ref[...]
    rates = jnp.broadcast_to(rates_ref[...], (8, count))
    lanes = lax.dot_general(
        rates, place, (((1,), (0,)), ((), ())), precision=highest_degree,
        preferred_element_type=jnp.float32,
    )
    rate_ref[...] = lanes * rows_ref[3:4, :]


def mix_axial(value, rows_ref):
    down = pltpu.roll(value, 1, 1)
    up = pltpu.roll(value, LANES - 1, 1)
    return rows_ref[0:1, :] * down + rows_ref[1:2, :] * up


def cross_and_collide(lower, middle, upper, flags, rows_ref, rate_ref, cross_ref, table_ref, bound):
    high, low = split(upper - lower)
    pair = jnp.dot(
        jnp.concatenate([high, low], axis=1), cross_ref[...], preferred_element_type=jnp.float32
    )
    central = pair[:, :LANES] + pair[:, LANES:]
    moved = middle - cross_step * (
        0.5 * central - 0.5 * bound * (upper - 2.0 * middle + lower)
    )
    moved = moved * (1.0 - flags * rows_ref[2:3, :])
    high, low = split(moved)
    sums = jnp.dot(
        jnp.concatenate([high, low], axis=1), table_ref[...], preferred_element_type=jnp.float32
    )
    mixing = sums[:, :LANES] + sums[:, LANES : 2 * LANES]
    target = rows_ref[4:5, :] * sums[:, 2 * LANES : 3 * LANES] * sums[:, 3 * LANES :]
    return moved + collide_step * (mixing - rate_ref[0:1, :] * (moved - target))


def march_kernel(
    held_ref, last_ref, deriv_ref, small_ref, rows_ref, rate_ref, cross_ref, table_ref,
    back_ref, out_ref, field, moved, after, ends, final, *, reach, chunk, bound
):
    me, slab = lax.axis_index("wa"), lax.axis_index("gy")
    cells, lines, flag_lane = out_ref.shape
    length = field.shape[1]
    rim_slot = jnp.where(slab == 0, lines + HALO, 0)
    half = held_ref.shape[0]
    for entry, offset in enumerate(reach):
        source = held_ref.at[entry] if entry < half else last_ref.at[entry - half]
        start = pl.multiple_of((me ^ offset) * cells, cells)
        field[HALO : HALO + lines, pl.ds(start, cells), :] = source[0:lines]
        field[pl.ds(rim_slot, HALO), pl.ds(start, cells), :] = source[lines:]

    zero = jnp.zeros((length, LANES), jnp.float32)
    moved[HALO - 1] = zero
    moved[HALO + lines] = zero
    first_slot = jnp.where(slab == 0, HALO, 0)
    width = 2
    total = lines + HALO
    for position in range(0, total, width):
        columns = [first_slot + position + k for k in range(min(width, total - position))]
        values = [field[column] for column in columns]
        high, low = split(jnp.concatenate(values, axis=1))
        series = jnp.dot(
            deriv_ref[...],
            jnp.concatenate([high, low, high], axis=0),
            preferred_element_type=jnp.float32,
        )
        for k, column in enumerate(columns):
            part = series[:, k * LANES : (k + 1) * LANES]
            term = part[(TERMS - 1) * length :]
            for n in range(TERMS - 2, -1, -1):
                term = part[n * length : (n + 1) * length] + mix_axial(term, rows_ref)
            moved[column] = values[k] + mix_axial(term, rows_ref)

    start_slot = HALO - slab
    total = lines + 1
    for position in range(0, total, chunk):
        size = min(chunk, total - position)
        base = start_slot + position
        flat = (size * length, LANES)
        lower = moved[pl.ds(base - 1, size)].reshape(flat)
        middle = moved[pl.ds(base, size)].reshape(flat)
        upper = moved[pl.ds(base + 1, size)].reshape(flat)
        flags = field[pl.ds(base, size)].reshape(flat)[:, flag_lane : flag_lane + 1]
        result = cross_and_collide(
            lower, middle, upper, flags, rows_ref, rate_ref, cross_ref, table_ref, bound
        )
        after[pl.ds(base, size)] = result.reshape(size, length, LANES)

    own = pl.multiple_of(me * cells, cells)
    taps = jnp.concatenate(
        [small_ref[pl.ds(n * length + own, cells), :] for n in range(TERMS)], axis=0
    )
    high, low = split(taps)
    taps = jnp.concatenate([high, high, low], axis=1)
    blank = jnp.zeros((cells, LANES), jnp.float32)
    ends[HALO - 1] = blank
    ends[HALO + lines] = blank
    for position in range(0, total, width):
        columns = [start_slot + position + k for k in range(min(width, total - position))]
        values = [after[column] for column in columns]
        high, low = split(jnp.concatenate(values, axis=1) if len(values) > 1 else values[0])
        series = jnp.dot(
            taps, jnp.concatenate([high, low, high], axis=0), preferred_element_type=jnp.float32
        )
        for k, column in enumerate(columns):
            part = series[:, k * LANES : (k + 1) * LANES]
            term = part[(TERMS - 1) * cells :]
            for n in range(TERMS - 2, -1, -1):
                term = part[n * cells : (n + 1) * cells] + mix_axial(term, rows_ref)
            ends[column] = after[column, pl.ds(own, cells), :] + mix_axial(term, rows_ref)

    flat = (lines * cells, LANES)
    flags = held_ref[0, 0:lines].reshape(flat)[:, flag_lane : flag_lane + 1]
    result = cross_and_collide(
        ends[HALO - 1 : HALO - 1 + lines].reshape(flat),
        ends[HALO : HALO + lines].reshape(flat),
        ends[HALO + 1 : HALO + 1 + lines].reshape(flat),
        flags, rows_ref, rate_ref, cross_ref, table_ref, bound,
    )
    final[...] = result.reshape(lines, cells, LANES)
    rows = jnp.concatenate([final[:, cell, :] for cell in range(cells)], axis=0)
    out_ref[...] = permute_lanes(rows, back_ref[...])[:, 0:flag_lane].reshape(out_ref.shape)


def gathered(input_moments, solid_cell_mask, collision_coefficients, relaxation_rates):
    count, cells, lines = input_moments.shape
    ranks = lax.axis_size("wa")
    length = cells * ranks
    place, rows, cross, first, second, band = lane_tables()
    bound = largest_root(DEG + 1)
    deriv = derivative_tables(length)
    deriv_high, deriv_low = halves(deriv)
    wide = np.concatenate([deriv_high, deriv_high, deriv_low], axis=1)
    cross_high, cross_low = halves(cross.T)
    cross_wide = np.block([[cross_high, cross_low], [cross_high, np.zeros_like(cross_low)]])
    picks = np.concatenate([first, second], axis=1).astype(bfloat)
    picks = np.concatenate([picks, picks], axis=0)
    vmem = pl.BlockSpec(memory_space=pltpu.VMEM)
    float32 = jnp.float32
    block, rim = pl.pallas_call(
        pack_kernel,
        out_shape=(
            jax.ShapeDtypeStruct((lines, cells, LANES), float32),
            jax.ShapeDtypeStruct((HALO, cells, LANES), float32),
        ),
        in_specs=[vmem] * 3,
        out_specs=(vmem, vmem),
        compiler_params=pltpu.CompilerParams(vmem_limit_bytes=8 * 2**20),
        name="pack",
    )(jnp.transpose(input_moments, (1, 2, 0)), solid_cell_mask, place.astype(bfloat))
    table, rate = pl.pallas_call(
        prepare_kernel,
        out_shape=(
            jax.ShapeDtypeStruct((2 * LANES, 4 * LANES), bfloat),
            jax.ShapeDtypeStruct((8, LANES), float32),
        ),
        in_specs=[vmem] * 6,
        out_specs=(vmem, vmem),
        compiler_params=pltpu.CompilerParams(vmem_limit_bytes=8 * 2**20),
        name="prepare",
    )(collision_coefficients, band, relaxation_rates.reshape(1, count), rows, place, picks)

    slabs = lax.axis_size("gy")
    rim = lax.ppermute(rim, "gy", [(i, i ^ 1) for i in range(slabs)])
    held = jnp.concatenate([block, rim], axis=0)[None]
    reach = [0]
    bit = ranks // 2
    while bit:
        got = lax.ppermute(held, "wa", [(i, i ^ bit) for i in range(ranks)])
        reach += [offset ^ bit for offset in reach]
        bit //= 2
        if bit:
            held = jnp.concatenate([held, got], axis=0)
    slots = lines + 2 * HALO
    result = pl.pallas_call(
        functools.partial(march_kernel, reach=tuple(reach), chunk=6, bound=bound),
        out_shape=jax.ShapeDtypeStruct((cells, lines, count), float32),
        in_specs=[vmem] * 9,
        out_specs=vmem,
        scratch_shapes=[
            pltpu.VMEM((slots, length, LANES), float32),
            pltpu.VMEM((slots, length, LANES), float32),
            pltpu.VMEM((slots, length, LANES), float32),
            pltpu.VMEM((slots, cells, LANES), float32),
            pltpu.VMEM((lines, cells, LANES), float32),
        ],
        compiler_params=pltpu.CompilerParams(vmem_limit_bytes=24 * 2**20),
        name="march",
    )(held, got, wide, deriv, rows, rate, cross_wide, table, place.T.astype(bfloat))
    return jnp.transpose(result, (2, 0, 1))


def gathers(sizes, shape):
    ranks, slabs = sizes["wa"], sizes["gy"]
    cells, lines = shape[1] // ranks, shape[2] // slabs
    slab_bytes = 4 * LANES * shape[1] * (lines + 2 * HALO)
    return (
        slabs == 2
        and ranks > 1
        and ranks & (ranks - 1) == 0
        and cells % 8 == 0
        and lines >= HALO
        and shape[0] < LANES
        and 6 * slab_bytes <= 40 * 2**20
    )


def solution(mesh):
    in_specs = (P(None, "wa", "gy"), P("wa", "gy"), P(), P())
    out_specs = P(None, "wa", "gy")

    def program(input_moments, *others):
        body = gathered if gathers(mesh.shape, input_moments.shape) else local
        mapped = jax.shard_map(
            body, mesh=mesh, in_specs=in_specs, out_specs=out_specs, check_vma=False
        )
        return mapped(input_moments, *others)

    return program
```

```python
import functools
import math

import jax
import jax.numpy as jnp
import numpy as np
from jax import lax
from jax.experimental import pallas as pl
from jax.experimental.pallas import tpu as pltpu
from jax.sharding import PartitionSpec as P

DEG = 7
ITERS = 2


highest_degree = lax.Precision.HIGHEST
axial_step = 0.2
cross_step = 0.2
collide_step = 0.5


def shifted(value, axis, by):
    count = lax.axis_size(axis)
    return lax.ppermute(value, axis, [(i, (i + by) % count) for i in range(count)])


def from_behind(value, axis, by):
    count = lax.axis_size(axis)
    pairs = [(i, i + by) for i in range(count) if 0 <= i + by < count]
    return lax.ppermute(value, axis, pairs)


def moment_table():
    entries = []
    for degree_now in range(DEG + 1):
        for first_k in range(degree_now, -1, -1):
            for second_k in range(degree_now - first_k, -1, -1):
                entries.append((first_k, second_k, degree_now - first_k - second_k))
    return entries


def hermite_value(order, point):
    previous = 1.0
    current_moments = point
    for level in range(1, order):
        previous, current_moments = (current_moments, point * current_moments - level * previous)
    return current_moments


def largest_root(order):
    upper = 2.0 * math.sqrt(order) + 1.0
    value_high = hermite_value(order, upper)
    lower = upper
    for trial in range(100000):
        lower = lower - 0.001
        value_low = hermite_value(order, lower)
        if (value_low > 0.0) != (value_high > 0.0):
            break
        upper = lower
        value_high = value_low
    for repeat in range(80):
        middle = 0.5 * (lower + upper)
        value_mid = hermite_value(order, middle)
        if (value_mid > 0.0) == (value_high > 0.0):
            upper = middle
            value_high = value_mid
        else:
            lower = middle
    return 0.5 * (lower + upper)


def coupling(entries, lookup, direction):
    matrix = np.zeros((len(entries), len(entries)), dtype=np.float32)
    for position, moment in enumerate(entries):
        raised = list(moment)
        raised[direction] += 1
        raised = tuple(raised)
        if raised in lookup:
            partner = lookup[raised]
            matrix[position, partner] = math.sqrt(moment[direction] + 1)
            matrix[partner, position] = math.sqrt(moment[direction] + 1)
    return matrix


def to_float(table):
    return jnp.asarray(table, dtype=jnp.float32)


def operator_tables():
    entries = moment_table()
    number = len(entries)
    lookup = {moment: position for position, moment in enumerate(entries)}
    axial_matrix = coupling(entries, lookup, 0)
    cross_matrix = coupling(entries, lookup, 1)
    degrees = np.array([sum(moment) for moment in entries])
    degree_band_mask = (
        (np.abs(degrees[:, None] - degrees[None, :]) <= 1)
        & (degrees[:, None] >= 2)
        & (degrees[None, :] >= 2)
    ).astype(np.float32)
    unit_rows = [lookup[1, 0, 0], lookup[0, 1, 0], lookup[0, 0, 1]]
    first_selection = np.zeros((number, number), dtype=np.float32)
    second_selection = np.zeros((number, number), dtype=np.float32)
    moment_weights = np.zeros(number, dtype=np.float32)
    for position, moment in enumerate(entries):
        if sum(moment) == 2:
            raised = [direction for direction in range(3) for repeat in range(moment[direction])]
            first_selection[position, unit_rows[raised[0]]] = 1.0
            second_selection[position, unit_rows[raised[1]]] = 1.0
            moment_weights[position] = 1.0 / math.sqrt(2.0) if raised[0] == raised[1] else 1.0
    relaxed = (degrees >= 2).astype(np.float32)
    density = (degrees == 0).astype(np.float32)
    speed_bound = largest_root(DEG + 1)
    return (
        to_float(axial_matrix),
        to_float(cross_matrix),
        to_float(degree_band_mask),
        to_float(first_selection),
        to_float(second_selection),
        to_float(moment_weights),
        to_float(relaxed),
        to_float(density),
        speed_bound,
    )


def wave_numbers(length):
    position = jnp.arange(length, dtype=jnp.int32)
    signed = jnp.where(position < length // 2, position, position - length)
    return signed.astype(jnp.float32) * (axial_step * 2.0 * math.pi / length)


def fourier_tables(length):
    position = jnp.arange(length, dtype=jnp.int32)
    phase_index = position[:, None] * position[None, :] % length
    angles = phase_index.astype(jnp.float32) * (2.0 * math.pi / length)
    return (jnp.cos(angles), jnp.sin(angles))


def phase_series(real_part, imag_part, axial_matrix, wave_scale):
    total_real, total_imag = (real_part, imag_part)
    term_real, term_imag = (real_part, imag_part)
    for term_order in range(1, 5):
        pushed_real = (
            jnp.einsum("js,suv->juv", axial_matrix, term_real, precision=highest_degree)
            * wave_scale[None, :, None]
        )
        pushed_imag = (
            jnp.einsum("js,suv->juv", axial_matrix, term_imag, precision=highest_degree)
            * wave_scale[None, :, None]
        )
        term_real, term_imag = (pushed_imag / term_order, -pushed_real / term_order)
        total_real = total_real + term_real
        total_imag = total_imag + term_imag
    return (total_real, total_imag)


def axial_update(line_field, cosine_table, sine_table, axial_matrix, wave_scale):
    length = line_field.shape[1]
    real_part = jnp.einsum("mxl,xk->mkl", line_field, cosine_table, precision=highest_degree)
    imag_part = -jnp.einsum("mxl,xk->mkl", line_field, sine_table, precision=highest_degree)
    total_real, total_imag = phase_series(real_part, imag_part, axial_matrix, wave_scale)
    restored = jnp.einsum("mkl,kx->mxl", total_real, cosine_table, precision=highest_degree)
    restored = restored - jnp.einsum(
        "mkl,kx->mxl", total_imag, sine_table, precision=highest_degree
    )
    return restored / length


def cross_update(current_moments, lower_rim, upper_rim, cross_matrix, speed_bound):
    central = jnp.einsum(
        "js,suv->juv", cross_matrix, upper_rim - lower_rim, precision=highest_degree
    )
    return current_moments - cross_step * (
        0.5 * central - 0.5 * speed_bound * (upper_rim - 2.0 * current_moments + lower_rim)
    )


def apply_walls(current_moments, mask_float, density):
    return current_moments * (1.0 - mask_float[None, :, :] * (1.0 - density)[:, None, None])


def apply_collisions(
    current_moments,
    collision_band,
    first_selection,
    second_selection,
    moment_weights,
    relaxation_applied,
):
    first_part = jnp.einsum(
        "js,suv->juv", first_selection, current_moments, precision=highest_degree
    )
    second_part = jnp.einsum(
        "js,suv->juv", second_selection, current_moments, precision=highest_degree
    )
    target = moment_weights[:, None, None] * first_part * second_part
    moment_mixing = jnp.einsum(
        "js,suv->juv", collision_band, current_moments, precision=highest_degree
    )
    return current_moments + collide_step * (
        moment_mixing - relaxation_applied[:, None, None] * (current_moments - target)
    )


def local(input_moments, solid_cell_mask, collision_coefficients, relaxation_rates):
    (
        axial_matrix,
        cross_matrix,
        degree_band_mask,
        first_selection,
        second_selection,
        moment_weights,
        relaxed,
        density,
        speed_bound,
    ) = operator_tables()
    collision_band = collision_coefficients * degree_band_mask
    relaxation_applied = relaxation_rates * relaxed
    length = input_moments.shape[1] * lax.axis_size("wa")
    cosine_table, sine_table = fourier_tables(length)
    wave_scale = wave_numbers(length)
    line_field = lax.all_to_all(input_moments, "wa", split_axis=2, concat_axis=1, tiled=True)
    mask_float = lax.all_to_all(
        solid_cell_mask, "wa", split_axis=1, concat_axis=0, tiled=True
    ).astype(jnp.float32)
    position_wa = lax.axis_index("wa")
    last_wa = lax.axis_size("wa") - 1
    for step_index in range(ITERS):
        line_field = axial_update(line_field, cosine_table, sine_table, axial_matrix, wave_scale)
        from_lower = shifted(line_field[:, :, -1:], "wa", 1)
        across_lower = from_behind(from_lower, "gy", 1)
        lower_line = jnp.where(position_wa == 0, across_lower, from_lower)
        from_upper = shifted(line_field[:, :, :1], "wa", -1)
        across_upper = from_behind(from_upper, "gy", -1)
        upper_line = jnp.where(position_wa == last_wa, across_upper, from_upper)
        padded = jnp.concatenate([lower_line, line_field, upper_line], axis=2)
        line_field = cross_update(
            line_field, padded[:, :, :-2], padded[:, :, 2:], cross_matrix, speed_bound
        )
        line_field = apply_walls(line_field, mask_float, density)
        line_field = apply_collisions(
            line_field,
            collision_band,
            first_selection,
            second_selection,
            moment_weights,
            relaxation_applied,
        )
    return lax.all_to_all(line_field, "wa", split_axis=1, concat_axis=2, tiled=True)


LANES = 128
HALO = ITERS
TERMS = 4
STRIDE = 8
CHUNK = 6
GROUP = 4
bfloat = jnp.bfloat16


def lane_tables():
    entries = moment_table()
    number = len(entries)
    lookup = {moment: position for position, moment in enumerate(entries)}
    height = -(-number // STRIDE)
    filled = [0] * STRIDE
    lane_of = {}
    for second_k, third_k in sorted({k[1:] for k in entries}, key=lambda k: (sum(k), k)):
        span = DEG + 1 - second_k - third_k
        column = next(c for c in range(STRIDE) if filled[c] + span <= height)
        for first_k in range(span):
            lane_of[first_k, second_k, third_k] = STRIDE * (filled[column] + first_k) + column
        filled[column] += span
    place = np.zeros((LANES, LANES), np.float32)
    for moment in entries:
        place[lookup[moment], lane_of[moment]] = 1.0
    place[number, number] = 1.0
    rows = np.zeros((8, LANES), np.float32)
    for moment in entries:
        lane = lane_of[moment]
        rows[0, lane] = math.sqrt(moment[0])
        if sum(moment) < DEG:
            rows[1, lane] = math.sqrt(moment[0] + 1)
        rows[2, lane] = 1.0 if sum(moment) > 0 else 0.0
        rows[3, lane] = 1.0 if sum(moment) >= 2 else 0.0
    cross = place[:number].T @ coupling(entries, lookup, 1) @ place[:number]
    first = np.zeros((LANES, LANES), np.float32)
    second = np.zeros((LANES, LANES), np.float32)
    units = [lane_of[1, 0, 0], lane_of[0, 1, 0], lane_of[0, 0, 1]]
    for moment in entries:
        if sum(moment) == 2:
            raised = [d for d in range(3) for repeat in range(moment[d])]
            first[units[raised[0]], lane_of[moment]] = 1.0
            second[units[raised[1]], lane_of[moment]] = 1.0
            rows[4, lane_of[moment]] = 1.0 / math.sqrt(2.0) if raised[0] == raised[1] else 1.0
    degrees = np.array([sum(moment) for moment in entries])
    band = (
        (np.abs(degrees[:, None] - degrees[None, :]) <= 1)
        & (degrees[:, None] >= 2)
        & (degrees[None, :] >= 2)
    ).astype(np.float32)
    return place, rows, cross, first, second, band


def halves(table):
    high = np.asarray(table, np.float32).astype(bfloat)
    low = (np.asarray(table, np.float32) - high.astype(np.float32)).astype(bfloat)
    return high, low


def split(value):
    high = value.astype(bfloat)
    low = (value - high.astype(jnp.float32)).astype(bfloat)
    return high, low


def derivative_tables(length):
    wave = np.arange(length)
    signed = np.where(wave < length // 2, wave, wave - length)
    scale = signed * (axial_step * 2.0 * math.pi / length)
    distance = np.arange(length)
    phase = np.exp(2j * np.pi * (wave[:, None] * distance[None, :] % length) / length)
    offset = (distance[:, None] - distance[None, :]) % length
    blocks = []
    for term in range(1, TERMS + 1):
        series = ((-1j * scale) ** term)[:, None] * phase / math.factorial(term)
        profile = series.sum(axis=0).real / length
        blocks.append(profile[offset])
    return np.concatenate(blocks, axis=0).astype(np.float32)


def thirds(value):
    high = value.astype(bfloat)
    rest = value - high.astype(jnp.float32)
    middle = rest.astype(bfloat)
    return high, middle, (rest - middle.astype(jnp.float32)).astype(bfloat)


def permute_lanes(value, place):
    total = None
    for part in thirds(value):
        moved = jnp.dot(part, place, preferred_element_type=jnp.float32)
        total = moved if total is None else total + moved
    return total


def pack_kernel(field_ref, mask_ref, place_ref, block_ref, rim_ref):
    cells, lines, count = field_ref.shape
    rows = field_ref[...].reshape(cells * lines, count)
    packed = permute_lanes(rows, place_ref[0:count, :])
    row = lax.broadcasted_iota(jnp.int32, (lines, lines), 0)
    column = lax.broadcasted_iota(jnp.int32, (lines, lines), 1)
    flags = jnp.concatenate(
        [
            jnp.where(row == column, mask_ref[cell : cell + 1, :].astype(jnp.float32), 0.0)
            for cell in range(cells)
        ],
        axis=0,
    )
    flag_row = jnp.broadcast_to(place_ref[count : count + 1, :], (lines, LANES))
    packed = packed + jnp.dot(flags.astype(bfloat), flag_row, preferred_element_type=jnp.float32)
    for cell in range(cells):
        block_ref[:, cell, :] = packed[cell * lines : (cell + 1) * lines]
    start = jnp.where(lax.axis_index("gy") == 0, lines - HALO, 0)
    rim_ref[...] = block_ref[pl.ds(start, HALO)]


def prepare_kernel(
    mixing_ref, band_ref, rates_ref, rows_ref, place_ref, select_ref, high_ref, low_ref, reach_ref,
    table_ref, rate_ref, deriv_ref, taps_ref
):
    count = mixing_ref.shape[0]
    cells = taps_ref.shape[0] // TERMS
    length = high_ref.shape[0]
    place = place_ref[0:count, :]
    banded = mixing_ref[...] * band_ref[...]
    half = lax.dot_general(
        banded, place, (((0,), (0,)), ((), ())), precision=highest_degree,
        preferred_element_type=jnp.float32,
    )
    mixed = lax.dot_general(
        place, half, (((0,), (0,)), ((), ())), precision=highest_degree,
        preferred_element_type=jnp.float32,
    )
    high, low = split(mixed)
    table_ref[0:LANES, 0:LANES] = high
    table_ref[LANES:, 0:LANES] = high
    table_ref[0:LANES, LANES : 2 * LANES] = low
    table_ref[LANES:, LANES : 2 * LANES] = jnp.zeros_like(low)
    table_ref[:, 2 * LANES :] = select_ref[...]
    rates = jnp.broadcast_to(rates_ref[...], (8, count))
    lanes = lax.dot_general(
        rates, place, (((1,), (0,)), ((), ())), precision=highest_degree,
        preferred_element_type=jnp.float32,
    )
    rate_ref[...] = lanes * rows_ref[3:4, :]

    me = lax.axis_index("wa")
    home = (me ^ reach_ref[...]) * cells
    row = lax.broadcasted_iota(jnp.int32, (length, length), 0) % cells
    column = lax.broadcasted_iota(jnp.int32, (length, length), 1)
    order = jnp.where(column == home + row, 1.0, 0.0).astype(bfloat)
    turned = []
    for source in (high_ref, low_ref):
        rows = jnp.dot(order, source[...], preferred_element_type=jnp.float32).astype(bfloat)
        blocks = [
            lax.dot_general(
                rows[:, n * length : (n + 1) * length], order, (((1,), (1,)), ((), ())),
                preferred_element_type=jnp.float32,
            )
            for n in range(TERMS)
        ]
        turned.append(jnp.concatenate(blocks, axis=1))
    high, low = [part.astype(bfloat) for part in turned]
    deriv_ref[...] = jnp.concatenate([high, high, low], axis=0)
    taps = []
    for n in range(TERMS):
        sign = 1.0 if n % 2 else -1.0
        span = slice(n * length, (n + 1) * length)
        high, low = sign * turned[0][0:cells, span], sign * turned[1][0:cells, span]
        taps.append(jnp.concatenate([high, high, low], axis=1))
    taps_ref[...] = jnp.concatenate(taps, axis=0).astype(bfloat)


def mix_axial(value, rows_ref):
    down = pltpu.roll(value, STRIDE, 1)
    up = pltpu.roll(value, LANES - STRIDE, 1)
    return rows_ref[0:1, :] * down + rows_ref[1:2, :] * up


def cross_and_collide(lower, middle, upper, flags, rows_ref, rate_ref, cross_ref, table_ref, bound):
    high, low = split(upper - lower)
    pair = jnp.dot(
        jnp.concatenate([high, low], axis=1), cross_ref[...], preferred_element_type=jnp.float32
    )
    central = pair[:, :LANES] + pair[:, LANES:]
    moved = middle - cross_step * (
        0.5 * central - 0.5 * bound * (upper - 2.0 * middle + lower)
    )
    moved = moved * (1.0 - flags * rows_ref[2:3, :])
    high, low = split(moved)
    sums = jnp.dot(
        jnp.concatenate([high, low], axis=1), table_ref[...], preferred_element_type=jnp.float32
    )
    mixing = sums[:, :LANES] + sums[:, LANES : 2 * LANES]
    target = rows_ref[4:5, :] * sums[:, 2 * LANES : 3 * LANES] * sums[:, 3 * LANES :]
    return moved + collide_step * (mixing - rate_ref[0:1, :] * (moved - target))


def march_kernel(
    held_ref, last_ref, deriv_ref, taps_ref, rows_ref, rate_ref, cross_ref, table_ref,
    shift_ref, back_ref, out_ref, moved, after, ends, final, *, chunk, group, bound
):
    slab = lax.axis_index("gy")
    cells, lines, flag_lane = out_ref.shape
    length = moved.shape[1]
    rim_slot = jnp.where(slab == 0, lines + HALO, 0)
    half = held_ref.shape[0]

    def mix_rows(value):
        size = value.shape[0] // LANES
        down = jnp.concatenate([value[-STRIDE:], value[:-STRIDE]], axis=0)
        up = jnp.concatenate([value[STRIDE:], value[:STRIDE]], axis=0)
        lower = jnp.concatenate([shift_ref[0:LANES]] * size, axis=0)
        upper = jnp.concatenate([shift_ref[LANES : 2 * LANES]] * size, axis=0)
        return lower * down + upper * up

    zero = jnp.zeros((length, LANES), jnp.float32)
    moved[HALO - 1] = zero
    moved[HALO + lines] = zero
    for position in range(0, lines + HALO, chunk):
        columns = list(range(position, min(position + chunk, lines + HALO)))
        turned = []
        for column in columns:
            blocks = [held_ref[entry, column] for entry in range(half)]
            blocks += [last_ref[entry, column] for entry in range(half)]
            turned.append(jnp.concatenate(blocks, axis=0).T)
        value = jnp.concatenate(turned, axis=0)
        high, low = split(value)
        series = jnp.dot(
            jnp.concatenate([high, low, high], axis=1), deriv_ref[...],
            preferred_element_type=jnp.float32,
        )
        term = series[:, (TERMS - 1) * length :]
        for n in range(TERMS - 2, -1, -1):
            term = series[:, n * length : (n + 1) * length] + mix_rows(term)
        value = value + mix_rows(term)
        for k, column in enumerate(columns):
            slot = HALO + column if column < lines else rim_slot + (column - lines)
            moved[slot] = value[k * LANES : (k + 1) * LANES].T

    start_slot = HALO - slab
    total = lines + 1
    for position in range(0, total, group):
        size = min(group, total - position)
        base = start_slot + position
        flat = (size * length, LANES)
        lower = moved[pl.ds(base - 1, size)].reshape(flat)
        middle = moved[pl.ds(base, size)].reshape(flat)
        upper = moved[pl.ds(base + 1, size)].reshape(flat)
        result = cross_and_collide(
            lower, middle, upper, middle[:, flag_lane : flag_lane + 1], rows_ref, rate_ref,
            cross_ref, table_ref, bound,
        )
        after[pl.ds(base, size)] = result.reshape(size, length, LANES)

    blank = jnp.zeros((cells, LANES), jnp.float32)
    ends[HALO - 1] = blank
    ends[HALO + lines] = blank
    parts = []
    for position in range(0, total, 2):
        slots = [start_slot + position + k for k in range(min(2, total - position))]
        high, low = split(jnp.concatenate([after[slot] for slot in slots], axis=1))
        series = jnp.dot(
            taps_ref[...], jnp.concatenate([high, low, high], axis=0),
            preferred_element_type=jnp.float32,
        )
        parts += [series[:, k * LANES : (k + 1) * LANES] for k in range(len(slots))]
    orders = [
        jnp.concatenate([part[n * cells : (n + 1) * cells] for part in parts], axis=0)
        for n in range(TERMS)
    ]
    term = orders.pop()
    while orders:
        term = orders.pop() + mix_axial(term, rows_ref)
    current = after[pl.ds(start_slot, total), 0:cells, :].reshape(total * cells, LANES)
    current = current + mix_axial(term, rows_ref)
    ends[pl.ds(start_slot, total)] = current.reshape(total, cells, LANES)

    flat = (lines * cells, LANES)
    flags = held_ref[0, 0:lines].reshape(flat)[:, flag_lane : flag_lane + 1]
    result = cross_and_collide(
        ends[HALO - 1 : HALO - 1 + lines].reshape(flat),
        ends[HALO : HALO + lines].reshape(flat),
        ends[HALO + 1 : HALO + 1 + lines].reshape(flat),
        flags, rows_ref, rate_ref, cross_ref, table_ref, bound,
    )
    final[...] = result.reshape(lines, cells, LANES)
    rows = jnp.concatenate([final[:, cell, :] for cell in range(cells)], axis=0)
    out_ref[...] = permute_lanes(rows, back_ref[...])[:, 0:flag_lane].reshape(out_ref.shape)


def gathered(input_moments, solid_cell_mask, collision_coefficients, relaxation_rates):
    count, cells, lines = input_moments.shape
    ranks = lax.axis_size("wa")
    length = cells * ranks
    place, rows, cross, first, second, band = lane_tables()
    bound = largest_root(DEG + 1)
    deriv = derivative_tables(length).reshape(TERMS, length, length)
    deriv_high, deriv_low = halves(np.concatenate([block.T for block in deriv], axis=1))
    reach = [0]
    bit = ranks // 2
    while bit:
        reach += [offset ^ bit for offset in reach]
        bit //= 2
    reach_rows = np.repeat(np.array(reach, np.int32), cells)[:, None]
    reach_rows = np.broadcast_to(reach_rows, (length, length))
    shift = np.concatenate(
        [np.broadcast_to(rows[k][:, None], (LANES, LANES)) for k in range(2)], axis=0
    )
    cross_high, cross_low = halves(cross.T)
    cross_wide = np.block([[cross_high, cross_low], [cross_high, np.zeros_like(cross_low)]])
    picks = np.concatenate([first, second], axis=1).astype(bfloat)
    picks = np.concatenate([picks, picks], axis=0)
    vmem = pl.BlockSpec(memory_space=pltpu.VMEM)
    float32 = jnp.float32
    block, rim = pl.pallas_call(
        pack_kernel,
        out_shape=(
            jax.ShapeDtypeStruct((lines, cells, LANES), float32),
            jax.ShapeDtypeStruct((HALO, cells, LANES), float32),
        ),
        in_specs=[vmem] * 3,
        out_specs=(vmem, vmem),
        compiler_params=pltpu.CompilerParams(vmem_limit_bytes=8 * 2**20),
        name="pack",
    )(jnp.transpose(input_moments, (1, 2, 0)), solid_cell_mask, place.astype(bfloat))
    table, rate, turned, taps = pl.pallas_call(
        prepare_kernel,
        out_shape=(
            jax.ShapeDtypeStruct((2 * LANES, 4 * LANES), bfloat),
            jax.ShapeDtypeStruct((8, LANES), float32),
            jax.ShapeDtypeStruct((3 * length, TERMS * length), bfloat),
            jax.ShapeDtypeStruct((TERMS * cells, 3 * length), bfloat),
        ),
        in_specs=[vmem] * 9,
        out_specs=(vmem,) * 4,
        compiler_params=pltpu.CompilerParams(vmem_limit_bytes=8 * 2**20),
        name="prepare",
    )(
        collision_coefficients, band, relaxation_rates.reshape(1, count), rows, place, picks,
        deriv_high, deriv_low, reach_rows,
    )

    slabs = lax.axis_size("gy")
    rim = lax.ppermute(rim, "gy", [(i, i ^ 1) for i in range(slabs)])
    held = jnp.concatenate([block, rim], axis=0)[None]
    bit = ranks // 2
    while bit:
        got = lax.ppermute(held, "wa", [(i, i ^ bit) for i in range(ranks)])
        bit //= 2
        if bit:
            held = jnp.concatenate([held, got], axis=0)
    slots = lines + 2 * HALO
    result = pl.pallas_call(
        functools.partial(march_kernel, chunk=CHUNK, group=GROUP, bound=bound),
        out_shape=jax.ShapeDtypeStruct((cells, lines, count), float32),
        in_specs=[vmem] * 10,
        out_specs=vmem,
        scratch_shapes=[
            pltpu.VMEM((slots, length, LANES), float32),
            pltpu.VMEM((slots, length, LANES), float32),
            pltpu.VMEM((slots, cells, LANES), float32),
            pltpu.VMEM((lines, cells, LANES), float32),
        ],
        compiler_params=pltpu.CompilerParams(vmem_limit_bytes=24 * 2**20),
        name="march",
    )(
        held, got, turned, taps, rows, rate, cross_wide, table, shift, place.T.astype(bfloat),
    )
    return jnp.transpose(result, (2, 0, 1))


def gathers(sizes, shape):
    ranks, slabs = sizes["wa"], sizes["gy"]
    cells, lines = shape[1] // ranks, shape[2] // slabs
    slab_bytes = 4 * LANES * shape[1] * (lines + 2 * HALO)
    return (
        slabs == 2
        and ranks > 1
        and ranks & (ranks - 1) == 0
        and cells == 8
        and shape[1] == LANES
        and lines >= HALO
        and shape[0] < LANES
        and 6 * slab_bytes <= 40 * 2**20
    )


def solution(mesh):
    in_specs = (P(None, "wa", "gy"), P("wa", "gy"), P(), P())
    out_specs = P(None, "wa", "gy")

    def program(input_moments, *others):
        body = gathered if gathers(mesh.shape, input_moments.shape) else local
        mapped = jax.shard_map(
            body, mesh=mesh, in_specs=in_specs, out_specs=out_specs, check_vma=False
        )
        return mapped(input_moments, *others)

    return program
```
